512 devices in a mesh: replica: 128 (over y, z_lo, x), dp: 4 (over z_hi, core).
Axes of the slice: x: 4, y: 4, z: 16 (z_hi: 2, z_lo: 8; z = z_hi * 8 + z_lo), core: 2. Of those that a mesh axis runs over, the one named last changes fastest.
Arguments:
- block_input: bfloat16 [1024, 288, 680], P(('replica', 'dp')), may hold values from -40 to 40
- time_shift: bfloat16 [1024, 680], P(('replica', 'dp')), may hold values from -4 to 4
- out_grad: bfloat16 [1024, 288, 680], P(('replica', 'dp')), may hold values from -6 to 6
- params: float32 [128, 680, 680], P('replica', 'dp'), may hold values from -0.21875 to 0.21875
- first_moment: float32 [128, 680, 680], P('replica', 'dp'), may hold values from -8 to 8
- second_moment: float32 [128, 680, 680], P('replica', 'dp'), may hold values from 1 to 20
- push_weight: float32 [128], P('replica'), may hold values from 0.5 to 2
- step: int32 [1], replicated, may hold values from 0 to 999
Outputs:
- grad_input: bfloat16 [1024, 288, 680], P(('replica', 'dp'))
- new_params: float32 [128, 680, 680], P('replica', 'dp')
- new_first: float32 [128, 680, 680], P('replica', 'dp')
- new_second: float32 [128, 680, 680], P('replica', 'dp')
- new_weight: float32 [128], P('replica')
The draws below stay inside these ranges and needn't reach their ends.
All inputs are finite; a program needn't handle non-finite values.
Results may differ from the reference program's by a relative error of at most 0.006.
Values may be sent and summed in bfloat16 or wider, within the bound.
A program may use at most 64 MiB of HBM per device.

```python
import math
import jax
import jax.numpy as jnp
from jax import lax

C = 680
GSIZE = 40
POS = 288
SAMPLES = 2
BATCH = 1024
N_REPLICA = 128
N_DP = 4


def draw_block_input(key, part):
    key_rows, key_chans, key_base = jax.random.split(key, 3)
    row_scale = jnp.exp(jax.random.uniform(key_rows, (BATCH, POS, 1), jnp.float32, 0.0, math.log(10.0)))
    channel_scale = jnp.exp(jax.random.uniform(key_chans, (1, 1, C), jnp.float32, 0.0, math.log(10.0)))
    multiplier = row_scale * channel_scale / 10.0
    drawn = jax.random.truncated_normal(key_base, -4.0, 4.0, (BATCH, POS, C), jnp.float32) * multiplier
    return drawn.astype(jnp.bfloat16)


def block_levels(stream_key, dims, shards, least, high):
    loudness = 1.0
    for position, blocks in shards:
        heights = jax.random.uniform(jax.random.fold_in(jax.random.fold_in(stream_key, 6), position), (blocks,), jnp.float32, least / len(shards), high / len(shards))
        loudness = loudness * jnp.repeat(jnp.exp(heights), dims[position] // blocks).reshape((-1,) + (1,) * (len(dims) - 1 - position))
    return loudness


def bell_draw(stream_key, shape, width, bound, cuts=(), kind=jnp.bfloat16):
    gain = block_levels(stream_key, shape, cuts, -0.22, 0.18) if cuts else 1.0
    entries = jax.random.normal(stream_key, shape, jnp.float32) * width * gain
    return jnp.minimum(jnp.maximum(entries, -bound), bound).astype(kind)


def setup_inputs(seed: int = 0) -> dict:
    streams_of = jax.random.split(jax.random.key(seed), 9)
    block_input = draw_block_input(jax.random.fold_in(streams_of[8], 71), 0)
    time_shift = bell_draw(streams_of[1], (BATCH, C), 1.0, 4.0, ((0, 512),))
    out_grad = bell_draw(streams_of[2], (BATCH, POS, C), 1.0, 6.0, ((0, 512),))
    params = bell_draw(streams_of[3], (N_REPLICA, C, C), C ** -0.5, 0.21875, ((0, 128), (1, 4)), jnp.float32)
    first_moment = bell_draw(streams_of[4], (N_REPLICA, C, C), 2.0, 8.0, ((0, 128), (1, 4)), jnp.float32)
    second_moment = jnp.clip(jnp.exp(math.log(20.0) - 2.9957323 * jax.random.uniform(streams_of[5], (N_REPLICA, C, C), jnp.float32) ** block_levels(streams_of[5], (N_REPLICA, C, C), ((0, 128), (1, 4)), -0.2, 0.2)), 1.0, 20.0)
    push_weight = jnp.clip(jnp.exp(math.log(2.0) - 1.3862944 * jax.random.uniform(streams_of[6], (N_REPLICA,), jnp.float32) ** block_levels(streams_of[6], (N_REPLICA,), ((0, 128),), -0.2, 0.2)), 0.5, 2.0)
    step = jax.random.randint(streams_of[7], (1,), 0, 1000).astype(jnp.int32)
    return dict(block_input=block_input, time_shift=time_shift, out_grad=out_grad, params=params, first_moment=first_moment, second_moment=second_moment, push_weight=push_weight, step=step)


NORM_EPS = 1e-05
BETA_ONE = 0.9
BETA_TWO = 0.999
LEARN_RATE = 0.002
ADAM_EPS = 1e-08

def norm_stats(values):
    grouped = values.reshape(values.shape[0], values.shape[1], -1, GSIZE)
    average = lax.optimization_barrier(jnp.mean(grouped, axis=(1, 3), keepdims=True))
    centered = grouped - average
    variance = lax.optimization_barrier(jnp.mean(centered * centered, axis=(1, 3), keepdims=True))
    inverse = lax.rsqrt(variance + NORM_EPS)
    return ((centered * inverse).reshape(values.shape), inverse)

def norm_back(grad_val, normed, inverse):
    shape_full = grad_val.shape
    grouped = grad_val.reshape(shape_full[0], shape_full[1], -1, GSIZE)
    normed_grp = normed.reshape(grouped.shape)
    first_mean = lax.optimization_barrier(jnp.mean(grouped, axis=(1, 3), keepdims=True))
    second_mean = lax.optimization_barrier(jnp.mean(grouped * normed_grp, axis=(1, 3), keepdims=True))
    return (inverse * (grouped - first_mean - normed_grp * second_mean)).reshape(shape_full)

def silu_grad(values):
    sigmoid_v = jax.nn.sigmoid(values)
    return sigmoid_v * (1.0 + values * (1.0 - sigmoid_v))

def reference(block_input, time_shift, out_grad, params, first_moment, second_moment, push_weight, step):
    replica_samples = SAMPLES * N_DP

    def per_replica(replica):
        first_row = (replica * replica_samples).astype(jnp.int32)
        inputs = lax.dynamic_slice_in_dim(block_input, first_row, replica_samples, 0)
        shifts = lax.dynamic_slice_in_dim(time_shift, first_row, replica_samples, 0)
        out_grads = lax.dynamic_slice_in_dim(out_grad, first_row, replica_samples, 0)
        weight = (params[replica] / push_weight[replica]).astype(jnp.bfloat16)
        normed_in, inverse_in = norm_stats(inputs.astype(jnp.float32))
        activation = jax.nn.silu(normed_in).astype(jnp.bfloat16)
        flat_act = activation.reshape(-1, C)
        hidden = jnp.dot(flat_act, weight, preferred_element_type=jnp.float32).reshape(inputs.shape)
        hidden = hidden + shifts.astype(jnp.float32)[:, None, :]
        normed_mid, inverse_mid = norm_stats(hidden)
        grad_mid = out_grads.astype(jnp.float32) * silu_grad(normed_mid)
        grad_hidden = norm_back(grad_mid, normed_mid, inverse_mid).astype(jnp.bfloat16).reshape(-1, C)
        weight_grad = lax.dot_general(flat_act, grad_hidden, (((0,), (0,)), ((), ())), preferred_element_type=jnp.float32)
        grad_act = jnp.dot(grad_hidden, weight.T, preferred_element_type=jnp.float32).reshape(inputs.shape)
        grad_input = norm_back(grad_act * silu_grad(normed_in), normed_in, inverse_in).astype(jnp.bfloat16)
        return (grad_input, weight_grad / N_DP)
    grad_input, grad = lax.map(per_replica, jnp.arange(N_REPLICA, dtype=jnp.int32))
    grad_input = grad_input.reshape(BATCH, POS, C)
    step_count = (step[0] + 1).astype(jnp.float32)
    first_new = BETA_ONE * first_moment + (1.0 - BETA_ONE) * grad
    second_new = BETA_TWO * second_moment + (1.0 - BETA_TWO) * grad * grad
    update = LEARN_RATE * (first_new / (1.0 - jnp.power(BETA_ONE, step_count)))
    update = update / (jnp.sqrt(second_new / (1.0 - jnp.power(BETA_TWO, step_count))) + ADAM_EPS)
    moved = params - update
    level_count = N_REPLICA.bit_length() - 1
    distance = jnp.left_shift(jnp.ones((), jnp.int32), step[0] % level_count)
    source = (jnp.arange(N_REPLICA, dtype=jnp.int32) - distance) % N_REPLICA
    new_params = 0.5 * (moved + jnp.take(moved, source, axis=0))
    new_weight = 0.5 * (push_weight + jnp.take(push_weight, source, axis=0))
    return (grad_input, new_params, first_new, second_new, new_weight)
```

```python
import functools

import jax
import jax.numpy as jnp
from jax import lax
from jax.experimental import pallas as pl
from jax.experimental.pallas import tpu as pltpu
from jax.sharding import PartitionSpec as P

MESH = pl.DeviceIdType.MESH
F32 = jnp.float32
BF16 = jnp.bfloat16
HIGHEST = lax.Precision.HIGHEST

GSIZE = 40
NORM_EPS = 1e-05
BETA_ONE = 0.9
BETA_TWO = 0.999
LEARN_RATE = 0.002
ADAM_EPS = 1e-08

LANES = 128
USED = 120
SLOT = 176


def iota(shape, dim):
    return lax.broadcasted_iota(jnp.int32, shape, dim)


def dot(a, b, **kw):
    return jnp.dot(a, b, preferred_element_type=F32, **kw)


def dot_nt(a, b):
    return lax.dot_general(a, b, (((1,), (1,)), ((), ())), preferred_element_type=F32)


def sigmoid(v):
    return 0.5 * jnp.tanh(0.5 * v) + 0.5


def step_kernel(
    x_ref, shift_ref, og_ref, par_ref, mom_ref, sec_ref, push_ref, step_ref,
    gi_ref, moved_ref, send_ref, first_ref, second_ref,
    nat, wall, wnat, act, act_t, xn, dsil, ogg, tsg, gh, dw, dw_in, own, bsend, brecv,
    a_core_s, a_core_r, a_z_s, a_z_r, a_rel_s, a_rel_r, b_core_s, b_core_r, b_z_s, b_z_r,
):
    samples, positions, channels = x_ref.shape
    rows = par_ref.shape[0]
    tiles = wall.shape[0]
    tokens = samples * positions
    replica, dp = lax.axis_index("replica"), lax.axis_index("dp")
    far, core = dp // 2, lax.rem(dp, 2)
    partner = (replica, far * 2 + 1 - core)
    across = (replica, (1 - far) * 2 + core)
    mine, across_slot = core * 2 + far, core * 2 + 1 - far

    barrier = pltpu.get_barrier_semaphore()
    for peer in (partner, across):
        pl.semaphore_signal(barrier, inc=1, device_id=peer, device_id_type=MESH)

    def remote(src, dst, s, r, to):
        return pltpu.make_async_remote_copy(
            src_ref=src, dst_ref=dst, send_sem=s, recv_sem=r, device_id=to, device_id_type=MESH
        )

    def a_core(t):
        return remote(wall.at[t, mine], wall.at[t, mine], a_core_s.at[t], a_core_r.at[t], partner)

    def a_z(t):
        return remote(wall.at[t, mine], wall.at[t, mine], a_z_s.at[t], a_z_r.at[t], across)

    def a_rel(t):
        block = wall.at[t, across_slot]
        return remote(block, block, a_rel_s.at[t], a_rel_r.at[t], partner)

    def b_core(t):
        return remote(dw.at[t, 1 - core], dw_in.at[t], b_core_s.at[t], b_core_r.at[t], partner)

    def b_z(t):
        return remote(bsend.at[t], brecv.at[t], b_z_s.at[t], b_z_r.at[t], across)

    lane = iota((SLOT, LANES), 1)

    nat[...] = jnp.zeros_like(nat)
    nat[0:rows, 0:channels] = par_ref[...] / push_ref[0]
    pl.semaphore_wait(barrier, 2)
    for t in range(tiles):
        high = nat[:, t * LANES : (t + 1) * LANES]
        if t:
            low = nat[:, (t - 1) * LANES : t * LANES]
            tile = jnp.where(
                lane < 8 * t, pltpu.roll(low, 8 * t, 1), pltpu.roll(high, 8 * t, 1)
            )
        else:
            tile = high
        wall[t, mine] = jnp.where(lane < USED, tile, 0.0).astype(BF16)
        a_z(t).start()
        a_core(t).start()

    def group_of(index):
        total = jnp.zeros_like(index)
        for g in range(1, channels // GSIZE):
            total = total + (index >= g * GSIZE).astype(jnp.int32)
        return total

    to_group = (group_of(iota((channels, LANES), 0)) == iota((channels, LANES), 1)).astype(F32)
    from_group = (iota((LANES, channels), 0) == group_of(iota((LANES, channels), 1))).astype(F32)

    def spread(total):
        total = jnp.broadcast_to(total, (8, channels))
        return dot(dot(total, to_group, precision=HIGHEST), from_group, precision=HIGHEST)[0:1]

    entries = positions * GSIZE

    inverse_in = []
    for s in range(samples):
        values = x_ref[s].astype(F32)
        average = spread(jnp.sum(values, axis=0, keepdims=True)) / entries
        centered = values - average
        variance = spread(jnp.sum(centered * centered, axis=0, keepdims=True)) / entries
        inverse = lax.rsqrt(variance + NORM_EPS)
        inverse_in.append(inverse)
        normed = centered * inverse
        sig = sigmoid(normed)
        span = pl.ds(s * positions, positions)
        xn[span, :] = normed
        act[span, :] = (normed * sig).astype(BF16)
        dsil[span, :] = sig * (1.0 + normed * (1.0 - sig))

    def source_of(index):
        out = index
        for q, owner in enumerate((0, 2, 1, 3)):
            inside = (index >= q * SLOT) & (index < q * SLOT + rows)
            shifted = index - q * SLOT + owner * rows
            out = jnp.where(inside, shifted, out)
            out = jnp.where((index >= q * SLOT + rows) & (index < (q + 1) * SLOT), -1, out)
        return out

    padded = 4 * SLOT
    unpad = (iota((channels, padded), 0) == source_of(iota((channels, padded), 1))).astype(BF16)
    pad = (source_of(iota((padded, channels), 0)) == iota((padded, channels), 1)).astype(BF16)
    act_t[...] = dot_nt(pad, act[...]).astype(BF16)

    shifts = jnp.concatenate(
        [shift_ref[...].astype(F32), jnp.zeros((16 - samples, channels), F32)], axis=0
    ).astype(BF16)

    def regroup(t, _):
        column = iota((channels, LANES), 1)
        select = (iota((channels, LANES), 0) == column + t * USED) & (column < USED)
        select = select.astype(F32).astype(BF16)
        for s in range(samples):
            ogg[t, pl.ds(s * positions, positions), :] = dot(og_ref[s], select).astype(BF16)
        tsg[t] = dot(shifts, select)
        return 0

    lax.fori_loop(0, tiles, regroup, 0)

    row_t, col_t = iota((LANES, LANES), 0), iota((LANES, LANES), 1)
    group_row = sum((row_t >= g * GSIZE).astype(jnp.int32) for g in (1, 2, 3))
    group_col = sum((col_t >= g * GSIZE).astype(jnp.int32) for g in (1, 2, 3))
    same_group = (group_row == group_col).astype(F32)

    def tile_spread(total):
        return dot(jnp.broadcast_to(total, (8, LANES)), same_group, precision=HIGHEST)[0:1]

    def finish(t):
        b_core(t).wait_recv()
        bsend[t] = (dw[t, core, 1 - far] + dw_in[t, 1 - far]).astype(BF16)
        b_z(t).start()
        own[t] = dw[t, core, far] + dw_in[t, far]

    def relay(t):
        a_z(t).wait_recv()
        a_rel(t).start()

    relay(0)

    def tile_step(t, _):
        @pl.when(t + 1 < tiles)
        def _():
            relay(t + 1)

        a_core(t).wait_recv()
        a_rel(t).wait_recv()
        weight = dot(unpad, wall[t].reshape(padded, LANES)).astype(BF16)
        wnat[t] = weight
        for s in range(samples):
            span = pl.ds(s * positions, positions)
            hidden = dot(act[span, :], weight) + tsg[t, s : s + 1, :]
            average = tile_spread(jnp.sum(hidden, axis=0, keepdims=True)) / entries
            centered = hidden - average
            variance = tile_spread(jnp.sum(centered * centered, axis=0, keepdims=True)) / entries
            inverse = lax.rsqrt(variance + NORM_EPS)
            normed = centered * inverse
            sig = sigmoid(normed)
            grad_mid = ogg[t, span, :].astype(F32) * (sig * (1.0 + normed * (1.0 - sig)))
            mean_one = tile_spread(jnp.sum(grad_mid, axis=0, keepdims=True)) / entries
            mean_two = tile_spread(jnp.sum(grad_mid * normed, axis=0, keepdims=True)) / entries
            grad_hidden = inverse * (grad_mid - mean_one - normed * mean_two)
            gh[t, span, :] = grad_hidden.astype(BF16)
        dw[t] = dot(act_t[...], gh[t]).reshape(2, 2, SLOT, LANES)
        b_core(t).start()

        @pl.when(t > 0)
        def _():
            finish(t - 1)

        return 0

    lax.fori_loop(0, tiles, tile_step, 0)
    finish(tiles - 1)

    for s in range(samples):
        span = pl.ds(s * positions, positions)
        total = jnp.zeros((positions, channels), F32)
        for t in range(tiles):
            total = total + dot_nt(gh[t, span, :], wnat[t])
        grad_val = total * dsil[span, :]
        normed = xn[span, :]
        mean_one = spread(jnp.sum(grad_val, axis=0, keepdims=True)) / entries
        mean_two = spread(jnp.sum(grad_val * normed, axis=0, keepdims=True)) / entries
        gi_ref[s] = (inverse_in[s] * (grad_val - mean_one - normed * mean_two)).astype(BF16)

    count = jnp.full((1, LANES), (step_ref[0] + 1).astype(F32))
    fix_one = 1.0 - jnp.power(jnp.full((1, LANES), BETA_ONE, F32), count)
    fix_two = 1.0 - jnp.power(jnp.full((1, LANES), BETA_TWO, F32), count)

    for t in range(tiles):
        b_z(t).wait_recv()
        own[t] = 0.25 * (own[t] + brecv[t].astype(F32))
    for t in range(tiles):
        this = own[t]
        if t:
            this = pltpu.roll(this, LANES - 8 * t, 1)
        if t + 1 < tiles:
            after = pltpu.roll(own[t + 1], USED - 8 * t, 1)
            this = jnp.where(lane < USED - 8 * t, this, after)
        width = min(LANES, channels - t * LANES)
        cols = pl.ds(t * LANES, width)
        grad = this[0:rows, 0:width]
        first_new = BETA_ONE * mom_ref[:, cols] + (1.0 - BETA_ONE) * grad
        second_new = BETA_TWO * sec_ref[:, cols] + (1.0 - BETA_TWO) * grad * grad
        first_ref[:, cols] = first_new
        second_ref[:, cols] = second_new
        update = LEARN_RATE * (first_new / fix_one[:, 0:width])
        update = update / (jnp.sqrt(second_new / fix_two[:, 0:width]) + ADAM_EPS)
        moved = par_ref[:, cols] - update
        moved_ref[:, cols] = moved
        send_ref[0:rows, cols] = moved.astype(BF16)
        send_ref[rows:SLOT, cols] = jnp.full((SLOT - rows, width), push_ref[0], F32).astype(BF16)

    for t in range(tiles):
        for copy in (a_core(t), a_z(t), a_rel(t), b_core(t), b_z(t)):
            copy.wait_send()


def train_step(x, shift, out_grad, params, first, second, push, step):
    samples, positions, channels = x.shape
    rows = params.shape[0]
    tokens = samples * positions
    tiles = -(-channels // USED)
    vmem = pl.BlockSpec(memory_space=pltpu.VMEM)
    smem = pl.BlockSpec(memory_space=pltpu.SMEM)
    dma = pltpu.SemaphoreType.DMA((tiles,))
    square = jax.ShapeDtypeStruct((rows, channels), F32)
    return pl.pallas_call(
        step_kernel,
        out_shape=(
            jax.ShapeDtypeStruct(x.shape, BF16),
            square,
            jax.ShapeDtypeStruct((SLOT, channels), BF16),
            square,
            square,
        ),
        in_specs=[vmem] * 6 + [smem] * 2,
        out_specs=(vmem,) * 5,
        scratch_shapes=[
            pltpu.VMEM((SLOT, tiles * LANES), F32),
            pltpu.VMEM((tiles, 4, SLOT, LANES), BF16),
            pltpu.VMEM((tiles, channels, LANES), BF16),
            pltpu.VMEM((tokens, channels), BF16),
            pltpu.VMEM((4 * SLOT, tokens), BF16),
            pltpu.VMEM((tokens, channels), F32),
            pltpu.VMEM((tokens, channels), F32),
            pltpu.VMEM((tiles, tokens, LANES), BF16),
            pltpu.VMEM((tiles, 16, LANES), F32),
            pltpu.VMEM((tiles, tokens, LANES), BF16),
            pltpu.VMEM((tiles, 2, 2, SLOT, LANES), F32),
            pltpu.VMEM((tiles, 2, SLOT, LANES), F32),
            pltpu.VMEM((tiles, SLOT, LANES), F32),
            pltpu.VMEM((tiles, SLOT, LANES), BF16),
            pltpu.VMEM((tiles, SLOT, LANES), BF16),
        ]
        + [dma] * 10,
        compiler_params=pltpu.CompilerParams(collective_id=0, has_side_effects=True),
    )(x, shift, out_grad, params, first, second, push, step)


def from_behind(block, axis, distance):
    devices = range(lax.axis_size(axis))
    route = [((i - distance) % len(devices), i) for i in devices]
    return lax.ppermute(block, axis, route)


def local(
    block_input, time_shift, out_grad, params, first_moment, second_moment, push_weight, step
):
    rows = params.shape[1]
    grad_input, moved, payload, first_new, second_new = train_step(
        block_input, time_shift, out_grad, params[0], first_moment[0], second_moment[0],
        push_weight, step,
    )
    level_count = lax.axis_size("replica").bit_length() - 1
    branches = [
        functools.partial(from_behind, axis="replica", distance=1 << power)
        for power in range(level_count)
    ]
    arrived = lax.switch(step[0] % level_count, branches, payload).astype(F32)
    averaged = 0.5 * (moved + arrived[:rows])
    new_weight = 0.5 * (push_weight + arrived[rows, :1])
    return (grad_input, averaged[None], first_new[None], second_new[None], new_weight)


def solution(mesh):
    placed = (
        P(("replica", "dp"), None, None),
        P(("replica", "dp"), None),
        P(("replica", "dp"), None, None),
        P("replica", "dp", None),
        P("replica", "dp", None),
        P("replica", "dp", None),
        P("replica"),
        P(),
    )
    return jax.shard_map(
        local,
        mesh=mesh,
        in_specs=placed,
        out_specs=(
            P(("replica", "dp"), None, None),
            P("replica", "dp", None),
            P("replica", "dp", None),
            P("replica", "dp", None),
            P("replica"),
        ),
        check_vma=False,
    )
```

```python
import functools

import jax
import jax.numpy as jnp
from jax import lax
from jax.experimental import pallas as pl
from jax.experimental.pallas import tpu as pltpu
from jax.sharding import PartitionSpec as P

MESH = pl.DeviceIdType.MESH
F32 = jnp.float32
BF16 = jnp.bfloat16
HIGHEST = lax.Precision.HIGHEST

GSIZE = 40
NORM_EPS = 1e-05
BETA_ONE = 0.9
BETA_TWO = 0.999
LEARN_RATE = 0.002
ADAM_EPS = 1e-08

LANES = 128
USED = 120
REST = 64
SLOT = 176


def iota(shape, dim):
    return lax.broadcasted_iota(jnp.int32, shape, dim)


def dot(a, b, **kw):
    return jnp.dot(a, b, preferred_element_type=F32, **kw)


def dot_nt(a, b):
    return lax.dot_general(a, b, (((1,), (1,)), ((), ())), preferred_element_type=F32)


def sigmoid(v):
    return 0.5 * jnp.tanh(0.5 * v) + 0.5


def pack_rest(last):
    lane = iota((REST, LANES), 1)
    third = jnp.concatenate(
        [last[2 * REST :], jnp.zeros((3 * REST - SLOT, LANES), last.dtype)], axis=0
    )
    second = pltpu.roll(last[REST : 2 * REST], GSIZE, 1)
    third = pltpu.roll(third, 2 * GSIZE, 1)
    return jnp.where(lane < GSIZE, last[:REST], jnp.where(lane < 2 * GSIZE, second, third))


def unpack_rest(packed):
    second = pltpu.roll(packed, LANES - GSIZE, 1)
    third = pltpu.roll(packed, LANES - 2 * GSIZE, 1)
    whole = jnp.concatenate([packed, second, third[: SLOT - 2 * REST]], axis=0)
    return jnp.where(iota((SLOT, LANES), 1) < GSIZE, whole, 0.0)


def step_kernel(
    x_hbm, shift_ref, og_hbm, par_hbm, mom_hbm, sec_hbm, push_ref, step_ref,
    gi_ref, moved_ref, first_ref, second_ref, gsend,
    x_ref, og_ref, par_ref, mom_ref, sec_ref,
    nat, wall, wnat, wgrp, act, act_t, xn, dsil, ogg, tsg, gh, dw, dwn, dw_in, own, bsend, brecv,
    load,
    a_core_s, a_core_r, a_z_s, a_z_r, a_rel_s, a_rel_r, b_core_s, b_core_r, b_z_s, b_z_r,
):
    samples, positions, channels = x_ref.shape
    rows = par_ref.shape[0]
    tiles = wgrp.shape[0]
    last = tiles - 1
    replica, dp = lax.axis_index("replica"), lax.axis_index("dp")
    far, core = dp // 2, lax.rem(dp, 2)
    partner = (replica, far * 2 + 1 - core)
    across = (replica, (1 - far) * 2 + core)
    mine, across_slot = core * 2 + far, core * 2 + 1 - far

    loads = [
        pltpu.make_async_copy(source, target, load.at[n])
        for n, (source, target) in enumerate(
            (
                (par_hbm.at[:, 0, :], par_ref),
                (x_hbm, x_ref),
                (og_hbm, og_ref),
                (mom_hbm.at[:, 0, :], mom_ref),
                (sec_hbm.at[:, 0, :], sec_ref),
            )
        )
    ]
    for copy in loads:
        copy.start()

    barrier = pltpu.get_barrier_semaphore()
    for peer in (partner, across):
        pl.semaphore_signal(barrier, inc=1, device_id=peer, device_id_type=MESH)

    def remote(src, dst, s, r, to):
        return pltpu.make_async_remote_copy(
            src_ref=src, dst_ref=dst, send_sem=s, recv_sem=r, device_id=to, device_id_type=MESH
        )

    def part(ref, rest):
        return ref.at[pl.ds(0, REST)] if rest else ref

    def a_core(t, rest=False):
        block = part(wall.at[t, mine], rest)
        return remote(block, block, a_core_s.at[t], a_core_r.at[t], partner)

    def a_z(t, rest=False):
        block = part(wall.at[t, mine], rest)
        return remote(block, block, a_z_s.at[t], a_z_r.at[t], across)

    def a_rel(t, rest=False):
        block = part(wall.at[t, across_slot], rest)
        return remote(block, block, a_rel_s.at[t], a_rel_r.at[t], partner)

    def b_core(t):
        return remote(dwn.at[t, 1 - core], dw_in.at[t], b_core_s.at[t], b_core_r.at[t], partner)

    def b_z(t, rest=False):
        return remote(
            part(bsend.at[t], rest), part(brecv.at[t], rest), b_z_s.at[t], b_z_r.at[t], across
        )

    lane = iota((SLOT, LANES), 1)

    nat[SLOT - 8 : SLOT, :] = jnp.zeros((8, nat.shape[1]), F32)
    nat[:, last * LANES :] = jnp.zeros((SLOT, LANES), F32)
    loads[0].wait()
    nat[0:rows, 0:channels] = par_ref[...] / push_ref[0]
    pl.semaphore_wait(barrier, 2)
    for t in range(last):
        wall[t, mine] = nat[:, t * LANES : (t + 1) * LANES].astype(BF16)
        a_z(t).start()
        a_core(t).start()
    wall[last, mine, 0:REST] = pack_rest(nat[:, last * LANES :]).astype(BF16)
    a_z(last, True).start()
    a_core(last, True).start()

    def group_of(index):
        total = jnp.zeros_like(index)
        for g in range(1, channels // GSIZE):
            total = total + (index >= g * GSIZE).astype(jnp.int32)
        return total

    to_group = (group_of(iota((channels, LANES), 0)) == iota((channels, LANES), 1)).astype(F32)
    from_group = (iota((LANES, channels), 0) == group_of(iota((LANES, channels), 1))).astype(F32)

    def stack(totals, width):
        row = iota((8, width), 0)
        out = jnp.zeros((8, width), F32)
        for n, total in enumerate(totals):
            out = jnp.where(row == n, total, out)
        return out

    def spread(totals):
        total = stack(totals, channels)
        return dot(dot(total, to_group, precision=HIGHEST), from_group, precision=HIGHEST) / entries

    def column_sum(values):
        return jnp.sum(values, axis=0, keepdims=True)

    entries = positions * GSIZE
    spans = [pl.ds(s * positions, positions) for s in range(samples)]

    loads[1].wait()
    average = spread([column_sum(x_ref[s].astype(F32)) for s in range(samples)])
    squares = []
    for s in range(samples):
        centered = x_ref[s].astype(F32) - average[s : s + 1]
        xn[spans[s], :] = centered
        squares.append(column_sum(centered * centered))
    inverse_in = lax.rsqrt(spread(squares) + NORM_EPS)
    for s in range(samples):
        normed = xn[spans[s], :] * inverse_in[s : s + 1]
        sig = sigmoid(normed)
        xn[spans[s], :] = normed
        act[spans[s], :] = (normed * sig).astype(BF16)
        dsil[spans[s], :] = sig * (1.0 + normed * (1.0 - sig))

    def source_of(index):
        out = index
        for q, owner in enumerate((0, 2, 1, 3)):
            inside = (index >= q * SLOT) & (index < q * SLOT + rows)
            shifted = index - q * SLOT + owner * rows
            out = jnp.where(inside, shifted, out)
            out = jnp.where((index >= q * SLOT + rows) & (index < (q + 1) * SLOT), -1, out)
        return out

    padded = 4 * SLOT
    unpad = (iota((channels, padded), 0) == source_of(iota((channels, padded), 1))).astype(BF16)
    pad = (source_of(iota((padded, channels), 0)) == iota((padded, channels), 1)).astype(BF16)
    act_t[...] = dot_nt(pad, act[...]).astype(BF16)

    shifts = jnp.concatenate(
        [shift_ref[...].astype(F32), jnp.zeros((16 - samples, channels), F32)], axis=0
    ).astype(BF16)

    loads[2].wait()

    def regroup(t, _):
        column = iota((channels, LANES), 1)
        select = (iota((channels, LANES), 0) == column + t * USED) & (column < USED)
        select = select.astype(F32).astype(BF16)
        for s in range(samples):
            ogg[t, spans[s], :] = dot(og_ref[s], select).astype(BF16)
        tsg[t] = dot(shifts, select)
        return 0

    lax.fori_loop(0, tiles, regroup, 0)

    lane8 = iota((8, LANES), 1)

    def tile_spread(totals):
        total = stack(totals, LANES) / entries
        sums = [
            jnp.sum(
                jnp.where((lane8 >= g * GSIZE) & (lane8 < (g + 1) * GSIZE), total, 0.0),
                axis=1,
                keepdims=True,
            )
            for g in range(3)
        ]
        return jnp.where(
            lane8 < GSIZE,
            sums[0],
            jnp.where(lane8 < 2 * GSIZE, sums[1], jnp.where(lane8 < USED, sums[2], 0.0)),
        )

    def to_natural(t, this, after):
        wide = this.shape
        column = iota(wide, 1)
        this = pltpu.roll(this, lax.rem(LANES - 8 * t, LANES), 1)
        after = pltpu.roll(after, USED - 8 * t, 1)
        return jnp.where(column < USED - 8 * t, this, after)

    def exchange(t, this, after):
        dwn[t] = to_natural(t, this, after).reshape(2, 2, SLOT, LANES)
        b_core(t).start()

    def finish(t, rest=False):
        b_core(t).wait_recv()
        away = dwn[t, core, 1 - far] + dw_in[t, 1 - far]
        if rest:
            bsend[t, 0:REST] = pack_rest(away).astype(BF16)
        else:
            bsend[t] = away.astype(BF16)
        b_z(t, rest).start()
        own[t] = dwn[t, core, far] + dw_in[t, far]

    def relay(t, rest=False):
        a_z(t, rest).wait_recv()
        a_rel(t, rest).start()

    relay(0)

    def tile_step(t, _):
        @pl.when(t + 1 < last)
        def _():
            relay(t + 1)

        @pl.when(t + 1 == last)
        def _():
            relay(last, True)

        @pl.when(t < last)
        def _():
            a_core(t).wait_recv()
            a_rel(t).wait_recv()

        @pl.when(t == last)
        def _():
            a_core(last, True).wait_recv()
            a_rel(last, True).wait_recv()
            for q in range(4):
                wall[tiles, q] = unpack_rest(wall[last, q, 0:REST].astype(F32)).astype(BF16)

        wide = (channels, LANES)
        column = iota(wide, 1)
        this = dot(unpad, wall[t + t // last].reshape(padded, LANES))
        wnat[lax.rem(t, 2)] = this
        before = wnat[lax.rem(t + 1, 2)]
        weight = jnp.where(
            column < 8 * t, pltpu.roll(before, 8 * t, 1), pltpu.roll(this, 8 * t, 1)
        )
        weight = jnp.where(column < USED, weight, 0.0).astype(BF16)
        wgrp[t] = weight

        hidden = [dot(act[span, :], weight) + tsg[t, s : s + 1, :] for s, span in enumerate(spans)]
        average = tile_spread([column_sum(h) for h in hidden])
        hidden = [h - average[s : s + 1] for s, h in enumerate(hidden)]
        variance = tile_spread([column_sum(h * h) for h in hidden])
        inverse = lax.rsqrt(variance + NORM_EPS)
        normed = [h * inverse[s : s + 1] for s, h in enumerate(hidden)]
        grads = []
        for s, n in enumerate(normed):
            sig = sigmoid(n)
            grads.append(ogg[t, spans[s], :].astype(F32) * (sig * (1.0 + n * (1.0 - sig))))
        means = tile_spread(
            [column_sum(g) for g in grads] + [column_sum(g * n) for g, n in zip(grads, normed)]
        )
        for s, (g, n) in enumerate(zip(grads, normed)):
            one, two = means[s : s + 1], means[samples + s : samples + s + 1]
            gh[t, spans[s], :] = (inverse[s : s + 1] * (g - one - n * two)).astype(BF16)

        now = lax.rem(t, 2)
        dw[now] = dot(act_t[...], gh[t])

        @pl.when(t > 0)
        def _():
            exchange(t - 1, dw[1 - now], dw[now])

        @pl.when(t > 1)
        def _():
            finish(t - 2)

        return 0

    wnat[1] = jnp.zeros((channels, LANES), F32)
    lax.fori_loop(0, tiles, tile_step, 0)
    exchange(last, dw[last % 2], dw[last % 2])
    finish(last - 1)

    sums_one, sums_two = [], []
    for s, span in enumerate(spans):
        total = jnp.zeros((positions, channels), F32)
        for t in range(tiles):
            total = total + dot_nt(gh[t, span, :], wgrp[t])
        grad_val = total * dsil[span, :]
        dsil[span, :] = grad_val
        sums_one.append(column_sum(grad_val))
        sums_two.append(column_sum(grad_val * xn[span, :]))
        if s == 0:
            finish(last, True)
    means = spread(sums_one + sums_two)
    for s, span in enumerate(spans):
        one, two = means[s : s + 1], means[samples + s : samples + s + 1]
        grad_val = dsil[span, :] - one - xn[span, :] * two
        gi_ref[s] = (inverse_in[s : s + 1] * grad_val).astype(BF16)

    count = jnp.full((1, LANES), (step_ref[0] + 1).astype(F32))
    fix_one = 1.0 - jnp.power(jnp.full((1, LANES), BETA_ONE, F32), count)
    fix_two = 1.0 - jnp.power(jnp.full((1, LANES), BETA_TWO, F32), count)
    loads[3].wait()
    loads[4].wait()
    extra = jnp.full((SLOT - rows, LANES), push_ref[0], F32)

    for t in range(tiles):
        rest = t == last
        width = min(LANES, channels - t * LANES)
        cols = pl.ds(t * LANES, width)
        b_z(t, rest).wait_recv()
        if rest:
            arrived = unpack_rest(brecv[t, 0:REST].astype(F32))
        else:
            arrived = brecv[t].astype(F32)
        grad = (0.25 * (own[t] + arrived))[0:rows, 0:width]
        first_new = BETA_ONE * mom_ref[:, cols] + (1.0 - BETA_ONE) * grad
        second_new = BETA_TWO * sec_ref[:, cols] + (1.0 - BETA_TWO) * grad * grad
        first_ref[:, cols] = first_new
        second_ref[:, cols] = second_new
        update = LEARN_RATE * (first_new / fix_one[:, 0:width])
        update = update / (jnp.sqrt(second_new / fix_two[:, 0:width]) + ADAM_EPS)
        moved = par_ref[:, cols] - update
        moved_ref[:, cols] = moved
        nat[0:rows, cols] = moved
        nat[rows:SLOT, t * LANES : (t + 1) * LANES] = extra
        moved = nat[:, t * LANES : (t + 1) * LANES]
        if rest:
            gsend[t, 0:REST] = pack_rest(moved).astype(BF16)
            gsend[t, REST:] = jnp.zeros((SLOT - REST, LANES), BF16)
        else:
            gsend[t] = moved.astype(BF16)

    for t in range(tiles):
        rest = t == last
        for copy in (a_core(t, rest), a_z(t, rest), a_rel(t, rest), b_z(t, rest)):
            copy.wait_send()
        b_core(t).wait_send()


def gossip_kernel(distance, send, arrived, send_sem, recv_sem):
    replica, dp = lax.axis_index("replica"), lax.axis_index("dp")
    replicas = lax.axis_size("replica")
    ahead = (lax.rem(replica + distance, replicas), dp)
    behind = (lax.rem(replica + replicas - distance, replicas), dp)
    barrier = pltpu.get_barrier_semaphore()
    pl.semaphore_signal(barrier, inc=1, device_id=behind, device_id_type=MESH)
    pl.semaphore_wait(barrier, 1)
    copy = pltpu.make_async_remote_copy(
        src_ref=send, dst_ref=arrived, send_sem=send_sem, recv_sem=recv_sem,
        device_id=ahead, device_id_type=MESH,
    )
    copy.start()
    copy.wait()


def gossip(distance, number, tiles):
    vmem = pl.BlockSpec(memory_space=pltpu.VMEM)
    return pl.pallas_call(
        functools.partial(gossip_kernel, distance),
        out_shape=jax.ShapeDtypeStruct(tiles.shape, BF16),
        in_specs=[vmem],
        out_specs=vmem,
        scratch_shapes=[pltpu.SemaphoreType.DMA, pltpu.SemaphoreType.DMA],
        compiler_params=pltpu.CompilerParams(
            collective_id=number, has_side_effects=True, vmem_limit_bytes=4 << 20
        ),
    )(tiles)


def output_kernel(
    gi_in, moved, first_in, second_in, near, push,
    gi_out, params_out, first_out, second_out, weight_out,
    average, sem,
):
    rows, channels = moved.shape
    tiles, last = near.shape[0], near.shape[0] - 1
    copies = [
        pltpu.make_async_copy(gi_in, gi_out, sem.at[0]),
        pltpu.make_async_copy(first_in, first_out.at[:, 0, :], sem.at[1]),
        pltpu.make_async_copy(second_in, second_out.at[:, 0, :], sem.at[2]),
        pltpu.make_async_copy(average, params_out.at[:, 0, :], sem.at[3]),
    ]
    for copy in copies[:3]:
        copy.start()
    for t in range(tiles):
        cols = pl.ds(t * LANES, min(LANES, channels - t * LANES))
        if t == last:
            arrived = unpack_rest(near[t, 0:REST].astype(F32))
        else:
            arrived = near[t].astype(F32)
        average[:, cols] = 0.5 * (moved[:, cols] + arrived[0:rows, 0 : cols.size])
        if t == 0:
            weight_out[...] = 0.5 * (push[0] + arrived[rows : rows + 1, :])
    copies[3].start()
    for copy in copies:
        copy.wait()


def write_out(grad_input, moved, first, second, near, push):
    rows, channels = moved.shape
    vmem = pl.BlockSpec(memory_space=pltpu.VMEM)
    hbm = pl.BlockSpec(memory_space=pltpu.HBM)
    square = jax.ShapeDtypeStruct((rows, 1, channels), F32)
    return pl.pallas_call(
        output_kernel,
        out_shape=(
            jax.ShapeDtypeStruct(grad_input.shape, BF16),
            square,
            square,
            square,
            jax.ShapeDtypeStruct((1, LANES), F32),
        ),
        in_specs=[vmem] * 5 + [pl.BlockSpec(memory_space=pltpu.SMEM)],
        out_specs=(hbm, hbm, hbm, hbm, vmem),
        scratch_shapes=[pltpu.VMEM((rows, channels), F32), pltpu.SemaphoreType.DMA((4,))],
        compiler_params=pltpu.CompilerParams(vmem_limit_bytes=16 << 20),
    )(grad_input, moved, first, second, near, push)


def pin(array):
    return pltpu.with_memory_space_constraint(array, pltpu.HBM)


def exchange_and_step(number, x, shift, out_grad, params, first, second, push, step):
    samples, positions, channels = x.shape
    rows = params.shape[0]
    tokens = samples * positions
    tiles = -(-channels // USED)
    vmem = pl.BlockSpec(memory_space=pltpu.VMEM)
    smem = pl.BlockSpec(memory_space=pltpu.SMEM)
    hbm = pl.BlockSpec(memory_space=pltpu.HBM)
    dma = pltpu.SemaphoreType.DMA((tiles,))
    square = jax.ShapeDtypeStruct((rows, channels), F32)
    tile = (SLOT, LANES)
    return pl.pallas_call(
        step_kernel,
        out_shape=(
            jax.ShapeDtypeStruct(x.shape, BF16),
            square,
            square,
            square,
            jax.ShapeDtypeStruct((tiles, *tile), BF16),
        ),
        in_specs=[hbm, vmem, hbm, hbm, hbm, hbm, smem, smem],
        out_specs=(vmem,) * 5,
        scratch_shapes=[
            pltpu.VMEM(x.shape, BF16),
            pltpu.VMEM(x.shape, BF16),
        ]
        + [pltpu.VMEM((rows, channels), F32)] * 3
        + [
            pltpu.VMEM((SLOT, tiles * LANES), F32),
            pltpu.VMEM((tiles + 1, 4, *tile), BF16),
            pltpu.VMEM((2, channels, LANES), F32),
            pltpu.VMEM((tiles, channels, LANES), BF16),
            pltpu.VMEM((tokens, channels), BF16),
            pltpu.VMEM((4 * SLOT, tokens), BF16),
            pltpu.VMEM((tokens, channels), F32),
            pltpu.VMEM((tokens, channels), F32),
            pltpu.VMEM((tiles, tokens, LANES), BF16),
            pltpu.VMEM((tiles, 16, LANES), F32),
            pltpu.VMEM((tiles, tokens, LANES), BF16),
            pltpu.VMEM((2, 4 * SLOT, LANES), F32),
            pltpu.VMEM((tiles, 2, 2, *tile), F32),
            pltpu.VMEM((tiles, 2, *tile), F32),
            pltpu.VMEM((tiles, *tile), F32),
        ]
        + [pltpu.VMEM((tiles, *tile), BF16)] * 2
        + [pltpu.SemaphoreType.DMA((5,))]
        + [dma] * 10,
        compiler_params=pltpu.CompilerParams(
            collective_id=number, has_side_effects=True, vmem_limit_bytes=40 << 20
        ),
    )(pin(x), shift, pin(out_grad), pin(params), pin(first), pin(second), push, step)


def local(
    block_input, time_shift, out_grad, params, first_moment, second_moment, push_weight, step
):
    def by_row(state):
        return jnp.transpose(state, (1, 0, 2))

    level_count = lax.axis_size("replica").bit_length() - 1
    grad_input, moved, first_new, second_new, tiles = exchange_and_step(
        level_count, block_input, time_shift, out_grad, by_row(params), by_row(first_moment),
        by_row(second_moment), push_weight, step,
    )
    branches = [functools.partial(gossip, 1 << power, power) for power in range(level_count)]
    near = lax.switch(step[0] % level_count, branches, tiles)
    grad_input, averaged, first_new, second_new, new_weight = write_out(
        grad_input, moved, first_new, second_new, near, push_weight
    )
    return (
        grad_input, by_row(averaged), by_row(first_new), by_row(second_new), new_weight[0, :1]
    )


def solution(mesh):
    placed = (
        P(("replica", "dp"), None, None),
        P(("replica", "dp"), None),
        P(("replica", "dp"), None, None),
        P("replica", "dp", None),
        P("replica", "dp", None),
        P("replica", "dp", None),
        P("replica"),
        P(),
    )
    return jax.shard_map(
        local,
        mesh=mesh,
        in_specs=placed,
        out_specs=(
            P(("replica", "dp"), None, None),
            P("replica", "dp", None),
            P("replica", "dp", None),
            P("replica", "dp", None),
            P("replica"),
        ),
        check_vma=False,
    )
```

```python
import functools

import jax
import jax.numpy as jnp
from jax import lax
from jax.experimental import pallas as pl
from jax.experimental.pallas import tpu as pltpu
from jax.sharding import PartitionSpec as P

MESH = pl.DeviceIdType.MESH
F32 = jnp.float32
BF16 = jnp.bfloat16
HIGHEST = lax.Precision.HIGHEST

GSIZE = 40
NORM_EPS = 1e-05
BETA_ONE = 0.9
BETA_TWO = 0.999
LEARN_RATE = 0.002
ADAM_EPS = 1e-08

LANES = 128
USED = 120
REST = 64
SLOT = 176


def iota(shape, dim):
    return lax.broadcasted_iota(jnp.int32, shape, dim)


def dot(a, b, **kw):
    return jnp.dot(a, b, preferred_element_type=F32, **kw)


def dot_nt(a, b):
    return lax.dot_general(a, b, (((1,), (1,)), ((), ())), preferred_element_type=F32)


def sigmoid(v):
    return 0.5 * jnp.tanh(0.5 * v) + 0.5


def pack_rest(last):
    lane = iota((REST, LANES), 1)
    third = jnp.concatenate(
        [last[2 * REST :], jnp.zeros((3 * REST - SLOT, LANES), last.dtype)], axis=0
    )
    second = pltpu.roll(last[REST : 2 * REST], GSIZE, 1)
    third = pltpu.roll(third, 2 * GSIZE, 1)
    return jnp.where(lane < GSIZE, last[:REST], jnp.where(lane < 2 * GSIZE, second, third))


def unpack_rest(packed):
    second = pltpu.roll(packed, LANES - GSIZE, 1)
    third = pltpu.roll(packed, LANES - 2 * GSIZE, 1)
    whole = jnp.concatenate([packed, second, third[: SLOT - 2 * REST]], axis=0)
    return jnp.where(iota((SLOT, LANES), 1) < GSIZE, whole, 0.0)


def step_kernel(
    x_hbm, shift_hbm, og_hbm, par_hbm, mom_hbm, sec_hbm, push_ref, step_ref,
    gi_ref, moved_ref, first_ref, second_ref, gsend,
    x_ref, shift_ref, og_ref, par_ref, mom_ref, sec_ref,
    nat, wall, wnat, wgrp, act, act_t, xn, dsil, ogg, tsg, gh, dw, dwn, dw_in, own, bsend, brecv,
    load,
    a_core_s, a_core_r, a_z_s, a_z_r, a_rel_s, a_rel_r, b_core_s, b_core_r, b_z_s, b_z_r,
):
    samples, positions, channels = x_ref.shape
    rows = par_ref.shape[0]
    tiles = wgrp.shape[0]
    last = tiles - 1
    replica, dp = lax.axis_index("replica"), lax.axis_index("dp")
    far, core = dp // 2, lax.rem(dp, 2)
    partner = (replica, far * 2 + 1 - core)
    across = (replica, (1 - far) * 2 + core)
    mine, across_slot = core * 2 + far, core * 2 + 1 - far

    loads = [
        pltpu.make_async_copy(source, target, load.at[n])
        for n, (source, target) in enumerate(
            (
                (par_hbm.at[:, 0, :], par_ref),
                (x_hbm, x_ref),
                (og_hbm, og_ref),
                (mom_hbm.at[:, 0, :], mom_ref),
                (sec_hbm.at[:, 0, :], sec_ref),
                (shift_hbm, shift_ref),
            )
        )
    ]
    for copy in loads:
        copy.start()

    barrier = pltpu.get_barrier_semaphore()
    for peer in (partner, across):
        pl.semaphore_signal(barrier, inc=1, device_id=peer, device_id_type=MESH)

    def remote(src, dst, s, r, to):
        return pltpu.make_async_remote_copy(
            src_ref=src, dst_ref=dst, send_sem=s, recv_sem=r, device_id=to, device_id_type=MESH
        )

    def part(ref, rest):
        return ref.at[pl.ds(0, REST)] if rest else ref

    def a_core(t, rest=False):
        block = part(wall.at[t, mine], rest)
        return remote(block, block, a_core_s.at[t], a_core_r.at[t], partner)

    def a_z(t, rest=False):
        block = part(wall.at[t, mine], rest)
        return remote(block, block, a_z_s.at[t], a_z_r.at[t], across)

    def a_rel(t, rest=False):
        block = part(wall.at[t, across_slot], rest)
        return remote(block, block, a_rel_s.at[t], a_rel_r.at[t], partner)

    def b_core(t):
        return remote(dwn.at[t, 1 - core], dw_in.at[t], b_core_s.at[t], b_core_r.at[t], partner)

    def b_z(t, rest=False):
        return remote(
            part(bsend.at[t], rest), part(brecv.at[t], rest), b_z_s.at[t], b_z_r.at[t], across
        )

    lane = iota((SLOT, LANES), 1)

    nat[SLOT - 8 : SLOT, :] = jnp.zeros((8, nat.shape[1]), F32)
    nat[:, last * LANES :] = jnp.zeros((SLOT, LANES), F32)
    loads[0].wait()
    nat[0:rows, 0:channels] = par_ref[...] / push_ref[0]
    pl.semaphore_wait(barrier, 2)
    for t in range(last):
        wall[t, mine] = nat[:, t * LANES : (t + 1) * LANES].astype(BF16)
        a_z(t).start()
        a_core(t).start()
    wall[last, mine, 0:REST] = pack_rest(nat[:, last * LANES :]).astype(BF16)
    a_z(last, True).start()
    a_core(last, True).start()

    def group_of(index):
        total = jnp.zeros_like(index)
        for g in range(1, channels // GSIZE):
            total = total + (index >= g * GSIZE).astype(jnp.int32)
        return total

    to_group = (group_of(iota((channels, LANES), 0)) == iota((channels, LANES), 1)).astype(F32)
    from_group = (iota((LANES, channels), 0) == group_of(iota((LANES, channels), 1))).astype(F32)

    def stack(totals, width):
        row = iota((8, width), 0)
        out = jnp.zeros((8, width), F32)
        for n, total in enumerate(totals):
            out = jnp.where(row == n, total, out)
        return out

    def spread(totals):
        total = stack(totals, channels)
        return dot(dot(total, to_group, precision=HIGHEST), from_group, precision=HIGHEST) / entries

    def column_sum(values):
        return jnp.sum(values, axis=0, keepdims=True)

    entries = positions * GSIZE
    spans = [pl.ds(s * positions, positions) for s in range(samples)]

    loads[1].wait()
    average = spread([column_sum(x_ref[s].astype(F32)) for s in range(samples)])
    squares = []
    for s in range(samples):
        centered = x_ref[s].astype(F32) - average[s : s + 1]
        xn[spans[s], :] = centered
        squares.append(column_sum(centered * centered))
    inverse_in = lax.rsqrt(spread(squares) + NORM_EPS)
    for s in range(samples):
        normed = xn[spans[s], :] * inverse_in[s : s + 1]
        sig = sigmoid(normed)
        xn[spans[s], :] = normed
        act[spans[s], :] = (normed * sig).astype(BF16)
        dsil[spans[s], :] = sig * (1.0 + normed * (1.0 - sig))

    def source_of(index):
        out = index
        for q, owner in enumerate((0, 2, 1, 3)):
            inside = (index >= q * SLOT) & (index < q * SLOT + rows)
            shifted = index - q * SLOT + owner * rows
            out = jnp.where(inside, shifted, out)
            out = jnp.where((index >= q * SLOT + rows) & (index < (q + 1) * SLOT), -1, out)
        return out

    padded = 4 * SLOT
    unpad = (iota((channels, padded), 0) == source_of(iota((channels, padded), 1))).astype(BF16)
    pad = (source_of(iota((padded, channels), 0)) == iota((padded, channels), 1)).astype(BF16)
    act_t[...] = dot_nt(pad, act[...]).astype(BF16)

    loads[5].wait()
    shifts = jnp.concatenate(
        [shift_ref[...].astype(F32), jnp.zeros((16 - samples, channels), F32)], axis=0
    ).astype(BF16)

    loads[2].wait()

    def regroup(t, _):
        column = iota((channels, LANES), 1)
        select = (iota((channels, LANES), 0) == column + t * USED) & (column < USED)
        select = select.astype(F32).astype(BF16)
        for s in range(samples):
            ogg[t, spans[s], :] = dot(og_ref[s], select).astype(BF16)
        tsg[t] = dot(shifts, select)
        return 0

    lax.fori_loop(0, tiles, regroup, 0)

    lane8 = iota((8, LANES), 1)

    def tile_spread(totals):
        total = stack(totals, LANES) / entries
        sums = [
            jnp.sum(
                jnp.where((lane8 >= g * GSIZE) & (lane8 < (g + 1) * GSIZE), total, 0.0),
                axis=1,
                keepdims=True,
            )
            for g in range(3)
        ]
        return jnp.where(
            lane8 < GSIZE,
            sums[0],
            jnp.where(lane8 < 2 * GSIZE, sums[1], jnp.where(lane8 < USED, sums[2], 0.0)),
        )

    def to_natural(t, this, after):
        wide = this.shape
        column = iota(wide, 1)
        this = pltpu.roll(this, lax.rem(LANES - 8 * t, LANES), 1)
        after = pltpu.roll(after, USED - 8 * t, 1)
        return jnp.where(column < USED - 8 * t, this, after)

    def exchange(t, this, after):
        dwn[t] = to_natural(t, this, after).reshape(2, 2, SLOT, LANES)
        b_core(t).start()

    def finish(t, rest=False):
        b_core(t).wait_recv()
        away = dwn[t, core, 1 - far] + dw_in[t, 1 - far]
        if rest:
            bsend[t, 0:REST] = pack_rest(away).astype(BF16)
        else:
            bsend[t] = away.astype(BF16)
        b_z(t, rest).start()
        own[t] = dwn[t, core, far] + dw_in[t, far]

    def relay(t, rest=False):
        a_z(t, rest).wait_recv()
        a_rel(t, rest).start()

    relay(0)

    def tile_step(t, _):
        @pl.when(t + 1 < last)
        def _():
            relay(t + 1)

        @pl.when(t + 1 == last)
        def _():
            relay(last, True)

        @pl.when(t < last)
        def _():
            a_core(t).wait_recv()
            a_rel(t).wait_recv()

        @pl.when(t == last)
        def _():
            a_core(last, True).wait_recv()
            a_rel(last, True).wait_recv()
            for q in range(4):
                wall[tiles, q] = unpack_rest(wall[last, q, 0:REST].astype(F32)).astype(BF16)

        wide = (channels, LANES)
        column = iota(wide, 1)
        this = dot(unpad, wall[t + t // last].reshape(padded, LANES))
        wnat[lax.rem(t, 2)] = this
        before = wnat[lax.rem(t + 1, 2)]
        weight = jnp.where(
            column < 8 * t, pltpu.roll(before, 8 * t, 1), pltpu.roll(this, 8 * t, 1)
        )
        weight = jnp.where(column < USED, weight, 0.0).astype(BF16)
        wgrp[t] = weight

        hidden = [dot(act[span, :], weight) + tsg[t, s : s + 1, :] for s, span in enumerate(spans)]
        average = tile_spread([column_sum(h) for h in hidden])
        hidden = [h - average[s : s + 1] for s, h in enumerate(hidden)]
        variance = tile_spread([column_sum(h * h) for h in hidden])
        inverse = lax.rsqrt(variance + NORM_EPS)
        normed = [h * inverse[s : s + 1] for s, h in enumerate(hidden)]
        grads = []
        for s, n in enumerate(normed):
            sig = sigmoid(n)
            grads.append(ogg[t, spans[s], :].astype(F32) * (sig * (1.0 + n * (1.0 - sig))))
        means = tile_spread(
            [column_sum(g) for g in grads] + [column_sum(g * n) for g, n in zip(grads, normed)]
        )
        for s, (g, n) in enumerate(zip(grads, normed)):
            one, two = means[s : s + 1], means[samples + s : samples + s + 1]
            gh[t, spans[s], :] = (inverse[s : s + 1] * (g - one - n * two)).astype(BF16)

        now = lax.rem(t, 2)
        dw[now] = dot(act_t[...], gh[t])

        @pl.when(t > 0)
        def _():
            exchange(t - 1, dw[1 - now], dw[now])

        @pl.when(t > 1)
        def _():
            finish(t - 2)

        return 0

    wnat[1] = jnp.zeros((channels, LANES), F32)
    lax.fori_loop(0, tiles, tile_step, 0)
    exchange(last, dw[last % 2], dw[last % 2])
    finish(last - 1)

    sums_one, sums_two = [], []
    for s, span in enumerate(spans):
        total = jnp.zeros((positions, channels), F32)
        for t in range(tiles):
            total = total + dot_nt(gh[t, span, :], wgrp[t])
        grad_val = total * dsil[span, :]
        dsil[span, :] = grad_val
        sums_one.append(column_sum(grad_val))
        sums_two.append(column_sum(grad_val * xn[span, :]))
        if s == 0:
            finish(last, True)
    means = spread(sums_one + sums_two)
    for s, span in enumerate(spans):
        one, two = means[s : s + 1], means[samples + s : samples + s + 1]
        grad_val = dsil[span, :] - one - xn[span, :] * two
        gi_ref[s] = (inverse_in[s : s + 1] * grad_val).astype(BF16)

    count = jnp.full((1, LANES), (step_ref[0] + 1).astype(F32))
    fix_one = 1.0 - jnp.power(jnp.full((1, LANES), BETA_ONE, F32), count)
    fix_two = 1.0 - jnp.power(jnp.full((1, LANES), BETA_TWO, F32), count)
    loads[3].wait()
    loads[4].wait()
    extra = jnp.full((SLOT - rows, LANES), push_ref[0], F32)

    for t in range(tiles):
        rest = t == last
        width = min(LANES, channels - t * LANES)
        cols = pl.ds(t * LANES, width)
        b_z(t, rest).wait_recv()
        if rest:
            arrived = unpack_rest(brecv[t, 0:REST].astype(F32))
        else:
            arrived = brecv[t].astype(F32)
        grad = (0.25 * (own[t] + arrived))[0:rows, 0:width]
        first_new = BETA_ONE * mom_ref[:, cols] + (1.0 - BETA_ONE) * grad
        second_new = BETA_TWO * sec_ref[:, cols] + (1.0 - BETA_TWO) * grad * grad
        first_ref[:, cols] = first_new
        second_ref[:, cols] = second_new
        update = LEARN_RATE * (first_new / fix_one[:, 0:width])
        update = update / (jnp.sqrt(second_new / fix_two[:, 0:width]) + ADAM_EPS)
        moved = par_ref[:, cols] - update
        moved_ref[:, cols] = moved
        nat[0:rows, cols] = moved
        nat[rows:SLOT, t * LANES : (t + 1) * LANES] = extra
        moved = nat[:, t * LANES : (t + 1) * LANES]
        if rest:
            gsend[t, 0:REST] = pack_rest(moved).astype(BF16)
        else:
            gsend[t] = moved.astype(BF16)

    for t in range(tiles):
        rest = t == last
        for copy in (a_core, a_z, a_rel, b_z):
            copy(t, rest).wait_send()
        b_core(t).wait_send()


def gossip_kernel(distance, send, arrived, send_sem, recv_sem):
    replica, dp = lax.axis_index("replica"), lax.axis_index("dp")
    replicas = lax.axis_size("replica")
    ahead = (lax.rem(replica + distance, replicas), dp)
    behind = (lax.rem(replica + replicas - distance, replicas), dp)
    barrier = pltpu.get_barrier_semaphore()
    pl.semaphore_signal(barrier, inc=1, device_id=behind, device_id_type=MESH)
    pl.semaphore_wait(barrier, 1)
    last = send.shape[0] - 1
    copies = [
        pltpu.make_async_remote_copy(
            src_ref=source, dst_ref=target, send_sem=send_sem.at[n], recv_sem=recv_sem.at[n],
            device_id=ahead, device_id_type=MESH,
        )
        for n, (source, target) in enumerate(
            (
                (send.at[pl.ds(0, last)], arrived.at[pl.ds(0, last)]),
                (send.at[last, pl.ds(0, REST)], arrived.at[last, pl.ds(0, REST)]),
            )
        )
    ]
    for copy in copies:
        copy.start()
    for copy in copies:
        copy.wait()


def gossip(distance, number, tiles):
    vmem = pl.BlockSpec(memory_space=pltpu.VMEM)
    return pl.pallas_call(
        functools.partial(gossip_kernel, distance),
        out_shape=jax.ShapeDtypeStruct(tiles.shape, BF16),
        in_specs=[vmem],
        out_specs=vmem,
        scratch_shapes=[pltpu.SemaphoreType.DMA((2,))] * 2,
        compiler_params=pltpu.CompilerParams(
            collective_id=number, has_side_effects=True, vmem_limit_bytes=4 << 20
        ),
    )(tiles)


def output_kernel(
    gi_in, moved, first_in, second_in, near, push,
    gi_out, params_out, first_out, second_out, weight_out,
    average, sem,
):
    rows, channels = moved.shape
    tiles, last = near.shape[0], near.shape[0] - 1
    copies = [
        pltpu.make_async_copy(gi_in, gi_out, sem.at[0]),
        pltpu.make_async_copy(first_in, first_out.at[:, 0, :], sem.at[1]),
        pltpu.make_async_copy(second_in, second_out.at[:, 0, :], sem.at[2]),
        pltpu.make_async_copy(average, params_out.at[:, 0, :], sem.at[3]),
    ]
    for copy in copies[:3]:
        copy.start()
    for t in range(tiles):
        cols = pl.ds(t * LANES, min(LANES, channels - t * LANES))
        if t == last:
            arrived = unpack_rest(near[t, 0:REST].astype(F32))
        else:
            arrived = near[t].astype(F32)
        average[:, cols] = 0.5 * (moved[:, cols] + arrived[0:rows, 0 : cols.size])
        if t == 0:
            weight_out[...] = 0.5 * (push[0] + arrived[rows : rows + 1, :])
    copies[3].start()
    for copy in copies:
        copy.wait()


def write_out(grad_input, moved, first, second, near, push):
    rows, channels = moved.shape
    vmem = pl.BlockSpec(memory_space=pltpu.VMEM)
    hbm = pl.BlockSpec(memory_space=pltpu.HBM)
    square = jax.ShapeDtypeStruct((rows, 1, channels), F32)
    return pl.pallas_call(
        output_kernel,
        out_shape=(
            jax.ShapeDtypeStruct(grad_input.shape, BF16),
            square,
            square,
            square,
            jax.ShapeDtypeStruct((1, LANES), F32),
        ),
        in_specs=[vmem] * 5 + [pl.BlockSpec(memory_space=pltpu.SMEM)],
        out_specs=(hbm, hbm, hbm, hbm, vmem),
        scratch_shapes=[pltpu.VMEM((rows, channels), F32), pltpu.SemaphoreType.DMA((4,))],
        compiler_params=pltpu.CompilerParams(vmem_limit_bytes=16 << 20),
    )(grad_input, moved, first, second, near, push)


def pin(array):
    return pltpu.with_memory_space_constraint(array, pltpu.HBM)


def exchange_and_step(number, x, shift, out_grad, params, first, second, push, step):
    samples, positions, channels = x.shape
    rows = params.shape[0]
    tokens = samples * positions
    tiles = -(-channels // USED)
    vmem = pl.BlockSpec(memory_space=pltpu.VMEM)
    smem = pl.BlockSpec(memory_space=pltpu.SMEM)
    hbm = pl.BlockSpec(memory_space=pltpu.HBM)
    dma = pltpu.SemaphoreType.DMA((tiles,))
    square = jax.ShapeDtypeStruct((rows, channels), F32)
    tile = (SLOT, LANES)
    return pl.pallas_call(
        step_kernel,
        out_shape=(
            jax.ShapeDtypeStruct(x.shape, BF16),
            square,
            square,
            square,
            jax.ShapeDtypeStruct((tiles, *tile), BF16),
        ),
        in_specs=[hbm] * 6 + [smem] * 2,
        out_specs=(vmem,) * 5,
        scratch_shapes=[
            pltpu.VMEM(x.shape, BF16),
            pltpu.VMEM(shift.shape, BF16),
            pltpu.VMEM(x.shape, BF16),
        ]
        + [pltpu.VMEM((rows, channels), F32)] * 3
        + [
            pltpu.VMEM((SLOT, tiles * LANES), F32),
            pltpu.VMEM((tiles + 1, 4, *tile), BF16),
            pltpu.VMEM((2, channels, LANES), F32),
            pltpu.VMEM((tiles, channels, LANES), BF16),
            pltpu.VMEM((tokens, channels), BF16),
            pltpu.VMEM((4 * SLOT, tokens), BF16),
            pltpu.VMEM((tokens, channels), F32),
            pltpu.VMEM((tokens, channels), F32),
            pltpu.VMEM((tiles, tokens, LANES), BF16),
            pltpu.VMEM((tiles, 16, LANES), F32),
            pltpu.VMEM((tiles, tokens, LANES), BF16),
            pltpu.VMEM((2, 4 * SLOT, LANES), F32),
            pltpu.VMEM((tiles, 2, 2, *tile), F32),
            pltpu.VMEM((tiles, 2, *tile), F32),
            pltpu.VMEM((tiles, *tile), F32),
        ]
        + [pltpu.VMEM((tiles, *tile), BF16)] * 2
        + [pltpu.SemaphoreType.DMA((6,))]
        + [dma] * 10,
        compiler_params=pltpu.CompilerParams(
            collective_id=number, has_side_effects=True, vmem_limit_bytes=40 << 20
        ),
    )(pin(x), pin(shift), pin(out_grad), pin(params), pin(first), pin(second), push, step)


def local(
    block_input, time_shift, out_grad, params, first_moment, second_moment, push_weight, step
):
    def by_row(state):
        return jnp.transpose(state, (1, 0, 2))

    level_count = lax.axis_size("replica").bit_length() - 1
    grad_input, moved, first_new, second_new, tiles = exchange_and_step(
        level_count, block_input, time_shift, out_grad, by_row(params), by_row(first_moment),
        by_row(second_moment), push_weight, step,
    )
    branches = [functools.partial(gossip, 1 << power, power) for power in range(level_count)]
    near = lax.switch(step[0] % level_count, branches, tiles)
    grad_input, averaged, first_new, second_new, new_weight = write_out(
        grad_input, moved, first_new, second_new, near, push_weight
    )
    return (
        grad_input, by_row(averaged), by_row(first_new), by_row(second_new), new_weight[0, :1]
    )


def solution(mesh):
    placed = (
        P(("replica", "dp"), None, None),
        P(("replica", "dp"), None),
        P(("replica", "dp"), None, None),
        P("replica", "dp", None),
        P("replica", "dp", None),
        P("replica", "dp", None),
        P("replica"),
        P(),
    )
    return jax.shard_map(
        local,
        mesh=mesh,
        in_specs=placed,
        out_specs=(
            P(("replica", "dp"), None, None),
            P("replica", "dp", None),
            P("replica", "dp", None),
            P("replica", "dp", None),
            P("replica"),
        ),
        check_vma=False,
    )
```
